32 devices in a mesh: row: 4 (over z), col: 8 (over y, x, core).
Axes of the slice: x: 2, y: 2, z: 4, core: 2. Of those that a mesh axis runs over, the one named last changes fastest.
Arguments:
- tokens: bfloat16 [256, 8192], P('col', 'row'), may hold values from -6 to 6
- out_grad: bfloat16 [256, 8192], P('col', 'row'), may hold values from -1.1953125 to 1.1953125
- w_gate: bfloat16 [8192, 16384], P('row', 'col'), may hold values from -0.0625 to 0.0625
- w_up: bfloat16 [8192, 16384], P('row', 'col'), may hold values from -0.0625 to 0.0625
- w_down: bfloat16 [16384, 8192], P('col', 'row'), may hold values from -0.046875 to 0.046875
Outputs:
- grad_input: bfloat16 [256, 8192], P('col', 'row')
- grad_gate: bfloat16 [8192, 16384], P('row', 'col')
- grad_up: bfloat16 [8192, 16384], P('row', 'col')
- grad_down: bfloat16 [16384, 8192], P('col', 'row')
The draws below stay inside these ranges and needn't reach their ends.
All inputs are finite; a program needn't handle non-finite values.
Results may differ from the reference program's by a relative error of at most 0.0049.
Values may be sent and summed in bfloat16 or wider, within the bound.
A program may use at most 128 MiB of HBM per device.

```python
import jax
import jax.numpy as jnp
from jax import lax

D = 8192
FF = 16384
TOKENS = 256


def strengthened(result, stream_key, source, target, shards_of, factor):
    def block_of(dim):
        return (jnp.arange(result.shape[dim]) // (result.shape[dim] // shards_of)).reshape((-1,) + (1,) * (result.ndim - 1 - dim))

    first = jax.random.permutation(stream_key, shards_of)[block_of(target)]
    second = (block_of(target) + shards_of // 2) % shards_of
    return jnp.where((block_of(source) == first) | (block_of(source) == second), factor * result, result)


def shard_levels(stream_key, shape, split, low, largest):
    def one(dim, parts):
        heights = jax.random.uniform(jax.random.fold_in(jax.random.fold_in(stream_key, 6), dim), (parts,), jnp.float32, low / len(split), largest / len(split))
        return jnp.repeat(jnp.exp(heights), shape[dim] // parts).reshape((-1,) + (1,) * (len(shape) - dim - 1))

    level = one(*split[0])
    for cut in split[1:]:
        level = level * one(*cut)
    return level


def gaussian(rng, shape, spread, reach, split=(), kind=jnp.bfloat16):
    gain = shard_levels(rng, shape, split, -0.22, 0.18) if split else 1.0
    drawn = jax.random.normal(rng, shape, jnp.float32) * spread * gain
    return jnp.minimum(jnp.maximum(drawn, -reach), reach).astype(kind)


def bell_draw_with(own_key, shape, spread, reach, shards, heavy, dtype=jnp.bfloat16):
    drawn = spread * jax.random.normal(own_key, shape, jnp.float32)
    if shards:
        drawn = drawn * shard_levels(own_key, shape, shards, -0.22, 0.18)
    return jnp.clip(strengthened(drawn, jax.random.fold_in(own_key, 3), *heavy), -reach, reach).astype(dtype)


def setup_inputs(seed: int = 0) -> dict:
    streams_of = jax.random.split(jax.random.key(seed), 6)
    tokens = bell_draw_with(streams_of[0], (TOKENS, D), 1.0, 6.0, ((0, 8), (1, 4)), (1, 0, 8, 2.0))
    out_grad = bell_draw_with(streams_of[1], (TOKENS, D), 0.2, 1.1953125, ((0, 8), (1, 4)), (1, 0, 8, 2.0))
    w_gate = gaussian(streams_of[2], (D, FF), D ** -0.5, 0.0625, ((0, 4), (1, 8)))
    w_up = gaussian(streams_of[3], (D, FF), D ** -0.5, 0.0625, ((0, 4), (1, 8)))
    w_down = gaussian(streams_of[4], (FF, D), FF ** -0.5, 0.046875, ((0, 8), (1, 4)))
    return dict(tokens=tokens, out_grad=out_grad, w_gate=w_gate, w_up=w_up, w_down=w_down)


def contract(left_array, right_array, left_dim, right_dim):
    return lax.dot_general(left_array, right_array, (((left_dim,), (right_dim,)), ((), ())), preferred_element_type=jnp.float32)


def swiglu_back(gate_sum, up_sum, hidden_grad):
    logistic = jax.nn.sigmoid(gate_sum)
    active = gate_sum * logistic
    hidden = (active * up_sum).astype(jnp.bfloat16)
    up_grad = (hidden_grad * active).astype(jnp.bfloat16)
    gate_grad = (hidden_grad * up_sum * logistic * (1.0 + gate_sum * (1.0 - logistic))).astype(jnp.bfloat16)
    return hidden, gate_grad, up_grad


def reference(tokens, out_grad, w_gate, w_up, w_down):
    gate_sum = jnp.dot(tokens, w_gate, preferred_element_type=jnp.float32)
    up_sum = jnp.dot(tokens, w_up, preferred_element_type=jnp.float32)
    hidden_grad = contract(out_grad, w_down, 1, 1)
    hidden, gate_grad, up_grad = swiglu_back(gate_sum, up_sum, hidden_grad)
    grad_down = contract(hidden, out_grad, 0, 0).astype(jnp.bfloat16)
    grad_gate = contract(tokens, gate_grad, 0, 0).astype(jnp.bfloat16)
    grad_up = contract(tokens, up_grad, 0, 0).astype(jnp.bfloat16)
    grad_input = (contract(gate_grad, w_gate, 1, 1) + contract(up_grad, w_up, 1, 1)).astype(jnp.bfloat16)
    return grad_input, grad_gate, grad_up, grad_down
```

```python
import functools

import jax
import jax.numpy as jnp
from jax import lax
from jax.experimental import pallas as pl
from jax.experimental.pallas import tpu as pltpu
from jax.sharding import PartitionSpec as P

BF16 = jnp.bfloat16
F32 = jnp.float32
MESH = pl.DeviceIdType.MESH


def contract(left_array, right_array, left_dim, right_dim):
    return lax.dot_general(
        left_array,
        right_array,
        (((left_dim,), (right_dim,)), ((), ())),
        preferred_element_type=F32,
    )


def swiglu_back(gate_sum, up_sum, hidden_grad):
    logistic = jax.nn.sigmoid(gate_sum)
    active = gate_sum * logistic
    hidden = (active * up_sum).astype(BF16)
    up_grad = (hidden_grad * active).astype(BF16)
    gate_grad = (hidden_grad * up_sum * logistic * (1.0 + gate_sum * (1.0 - logistic))).astype(BF16)
    return (hidden, gate_grad, up_grad)


def xor(a, b, size):
    total, bit = 0, 1
    while bit < size:
        p, q = (a // bit) % 2, (b // bit) % 2
        total = total + bit * (p + q - 2 * p * q)
        bit *= 2
    return total


def main_kernel(
    n, ncol, m, subs,
    x_hbm, g_hbm, wg_hbm, wu_hbm, wd_hbm,
    xa_out, ga_out, res_out, gi_out,
    xa, ga, wg, wu, wd, part, sent, inbox, res, share, pair, rs_src, rs_got,
    w_sem, own_sem, out_sem, res_sem,
    ag_send, ag_recv, in_send, in_recv, res_send, res_recv, pair_send, pair_recv, rs_send, rs_recv,
):
    row, col = lax.axis_index("row"), lax.axis_index("col")
    tl = x_hbm.shape[0]
    nb, _, t, fb = res.shape
    groups = ncol // 2
    gr = 2 * tl
    sr = gr // subs
    chunks = groups * nb
    core, chip = col % 2, col // 2
    sibling = col + 1 - 2 * core
    half = n // 2
    side = row // half
    place = row + side * (n - 1 - 2 * row)
    inner = row + 1 - 2 * side
    outer = row - 1 + 2 * side
    middle = place == half - 1

    def weight_copies(b):
        cols = pl.ds(pl.multiple_of(b * fb, fb), fb)
        return (
            pltpu.make_async_copy(wg_hbm.at[:, cols], wg.at[b], w_sem.at[0, b]),
            pltpu.make_async_copy(wu_hbm.at[:, cols], wu.at[b], w_sem.at[1, b]),
            pltpu.make_async_copy(wd_hbm.at[cols, :], wd.at[b], w_sem.at[2, b]),
        )

    def slot_rows(j, c):
        return pl.ds(pl.multiple_of(j * gr + c * tl, tl), tl)

    def group_rows(j):
        return pl.ds(pl.multiple_of(j * gr, gr), gr)

    def member(j, c):
        return (row, xor(chip, j, groups) * 2 + c)

    def own_copy(a):
        src, dst = ((x_hbm, xa), (g_hbm, ga))[a]
        return pltpu.make_async_copy(src, dst.at[slot_rows(0, core), :], own_sem.at[a])

    def gather_copy(a, j, to, source):
        src, dst = ((x_hbm, xa), (g_hbm, ga))[a]
        return pltpu.make_async_remote_copy(
            src_ref=src,
            dst_ref=dst.at[slot_rows(j, source), :],
            send_sem=ag_send.at[a, j, to],
            recv_sem=ag_recv.at[a, j, source],
            device_id=member(j, to),
            device_id_type=MESH,
        )

    barrier = pltpu.get_barrier_semaphore()
    pl.semaphore_signal(barrier, inc=1, device_id=(row, sibling), device_id_type=MESH)
    for j in range(1, groups):
        for c in range(2):
            pl.semaphore_signal(barrier, inc=1, device_id=member(j, c), device_id_type=MESH)
    pl.semaphore_signal(barrier, inc=1, device_id=(inner, col), device_id_type=MESH)

    @pl.when(place > 0)
    def _():
        pl.semaphore_signal(barrier, inc=1, device_id=(outer, col), device_id_type=MESH)

    for a in range(2):
        own_copy(a).start()
    for i in range(nb):
        for copy in weight_copies((i + nb - m) % nb):
            copy.start()
    share[...] = jnp.zeros_like(share)

    pl.semaphore_wait(barrier, ncol + (place + n - 1) // n)

    for a in range(2):
        gather_copy(a, 0, 1 - core, core).start()
    for j in range(1, groups):
        for a in range(2):
            for c in range(2):
                gather_copy(a, j, c, core).start()
    for a in range(2):
        own_copy(a).wait()
        gather_copy(a, 0, core, 1 - core).wait_recv()

    def spot(k):
        u = (k + nb - m) % chunks
        return u // nb, u % nb

    def in_copy(slot, k, s):
        rows = pl.ds(s * sr, sr)
        return pltpu.make_async_remote_copy(
            src_ref=sent.at[k, :, rows, :],
            dst_ref=inbox.at[slot, k, :, rows, :],
            send_sem=in_send.at[k, s],
            recv_sem=in_recv.at[slot, k, s],
            device_id=(inner, col),
            device_id_type=MESH,
        )

    def sub_rows(j, s):
        return pl.ds(pl.multiple_of(j * gr + s * sr, sr), sr)

    def res_copy(k, s):
        j, b = spot(k)
        block = res.at[b, :, sub_rows(j, s), :]
        return pltpu.make_async_remote_copy(
            src_ref=block,
            dst_ref=block,
            send_sem=res_send.at[k, s],
            recv_sem=res_recv.at[k, s],
            device_id=(outer, col),
            device_id_type=MESH,
        )

    def keep_copy(k):
        j, b = spot(k)
        rows = group_rows(j)
        return pltpu.make_async_copy(res.at[b, :, rows, :], res_out.at[b, :, rows, :], res_sem.at[k])

    def out_copy(a):
        return pltpu.make_async_copy((xa, ga)[a], (xa_out, ga_out)[a], out_sem.at[a])

    def pair_copy(j):
        return pltpu.make_async_remote_copy(
            src_ref=share.at[slot_rows(j, 1 - core), :],
            dst_ref=pair.at[j],
            send_sem=pair_send.at[j],
            recv_sem=pair_recv.at[j],
            device_id=(row, sibling),
            device_id_type=MESH,
        )

    def rs_copy(j):
        return pltpu.make_async_remote_copy(
            src_ref=rs_src.at[j],
            dst_ref=rs_got.at[j],
            send_sem=rs_send.at[j],
            recv_sem=rs_recv.at[j],
            device_id=member(j, core),
            device_id_type=MESH,
        )

    def send_sums(k, s):
        rows = pl.ds(s * sr, sr)
        for i in range(3):
            sent[k, i, rows, :] = part[k, i, rows, :].astype(BF16)
        in_copy((place + 1) // half, k, s).start()

    def forward(k):
        j, b = spot(k)

        @pl.when(k < nb)
        def _():
            for copy in weight_copies(b):
                copy.wait()

        @pl.when((b == 0) & (j > 0))
        def _():
            for a in range(2):
                for c in range(2):
                    gather_copy(a, j, core, c).wait_recv()

        @pl.when((b == 0) & (j == groups - 1))
        def _():
            for a in range(2):
                out_copy(a).start()

        x, g = xa[group_rows(j), :], ga[group_rows(j), :]
        part[k, 0] = jnp.dot(x, wg[b], preferred_element_type=F32)
        part[k, 1] = jnp.dot(x, wu[b], preferred_element_type=F32)
        part[k, 2] = contract(g, wd[b], 1, 1)

        @pl.when(place == 0)
        def _():
            for s in range(subs):
                send_sums(k, s)

    def accumulate(k):
        for s in range(subs):
            rows = pl.ds(s * sr, sr)
            in_copy(0, k, s).wait_recv()
            for i in range(3):
                part[k, i, rows, :] += inbox[0, k, i, rows, :].astype(F32)
            send_sums(k, s)

    def results(k):
        j, b = spot(k)
        for s in range(subs):
            rows = pl.ds(s * sr, sr)

            @pl.when(middle)
            def _():
                in_copy(1, k, s).wait_recv()
                values = swiglu_back(
                    *(part[k, i, rows, :] + inbox[1, k, i, rows, :].astype(F32) for i in range(3))
                )
                for i in range(3):
                    res[b, i, sub_rows(j, s), :] = values[i]

            @pl.when(place < half - 1)
            def _():
                res_copy(k, s).wait_recv()

            @pl.when(place > 0)
            def _():
                res_copy(k, s).start()

    def backward(k):
        j, b = spot(k)
        keep_copy(k).start()
        rows = group_rows(j)
        share[rows, :] += contract(res[b, 1, rows, :], wg[b], 1, 1) + contract(
            res[b, 2, rows, :], wu[b], 1, 1
        )

        @pl.when(((b == nb - 1) & (j > 0)) | (k == chunks - 1))
        def _():
            pair_copy(j).start()

    def pair_sum(j):
        pair_copy(j).wait_recv()
        return share[slot_rows(j, core), :] + pair[j]

    sum_lag = place
    res_lag = half + 2 * (half - 1 - place) + (half - 1 - place)

    def step(s, carry):
        @pl.when(s < chunks)
        def _():
            forward(s)

        k = s - sum_lag

        @pl.when((place > 0) & (k >= 0) & (k < chunks))
        def _():
            accumulate(k)

        r = s - res_lag

        @pl.when((r >= 0) & (r < chunks))
        def _():
            results(r)
            backward(r)

        before = r - 1
        j, b = spot(before + chunks)

        @pl.when((before >= 0) & (before < chunks) & (b == nb - 1) & (j > 0))
        def _():
            rs_src[j] = pair_sum(j).astype(BF16)
            rs_copy(j).start()

        return carry

    lax.fori_loop(0, chunks + half + 3 * (half - 1), step, 0)

    total = pair_sum(0)
    for j in range(1, groups):
        rs_copy(j).wait_recv()
        total += rs_got[j].astype(F32)
    gi_out[...] = total.astype(BF16)

    for a in range(2):
        out_copy(a).wait()
        gather_copy(a, 0, 1 - core, core).wait_send()
        for j in range(1, groups):
            for c in range(2):
                gather_copy(a, j, c, core).wait_send()
    for j in range(groups):
        pair_copy(j).wait_send()
        if j:
            rs_copy(j).wait_send()

    def drain(k, carry):
        keep_copy(k).wait()
        for s in range(subs):
            in_copy(0, k, s).wait_send()

            @pl.when(place > 0)
            def _():
                res_copy(k, s).wait_send()

        return carry

    lax.fori_loop(0, chunks, drain, 0)


def main_pass(n, ncol, tokens, out_grad, w_gate, w_up, w_down):
    tl, d = tokens.shape
    f = w_gate.shape[1]
    t = tl * ncol
    fb = min(256, f // 2)
    nb = f // fb
    m = max(1, nb * 5 // 8)
    groups, gr, subs = ncol // 2, 2 * tl, 2
    chunks = groups * nb
    vmem = pl.BlockSpec(memory_space=pltpu.VMEM)
    hbm = pl.BlockSpec(memory_space=pl.ANY)
    dma = pltpu.SemaphoreType.DMA
    return pl.pallas_call(
        functools.partial(main_kernel, n, ncol, m, subs),
        out_shape=[
            jax.ShapeDtypeStruct((t, d), BF16),
            jax.ShapeDtypeStruct((t, d), BF16),
            jax.ShapeDtypeStruct((nb, 3, t, fb), BF16),
            jax.ShapeDtypeStruct((tl, d), BF16),
        ],
        in_specs=[hbm] * 5,
        out_specs=[hbm, hbm, hbm, vmem],
        scratch_shapes=[
            pltpu.VMEM((t, d), BF16),
            pltpu.VMEM((t, d), BF16),
            pltpu.VMEM((nb, d, fb), BF16),
            pltpu.VMEM((nb, d, fb), BF16),
            pltpu.VMEM((nb, fb, d), BF16),
            pltpu.VMEM((chunks, 3, gr, fb), F32),
            pltpu.VMEM((chunks, 3, gr, fb), BF16),
            pltpu.VMEM((2, chunks, 3, gr, fb), BF16),
            pltpu.VMEM((nb, 3, t, fb), BF16),
            pltpu.VMEM((t, d), F32),
            pltpu.VMEM((groups, tl, d), F32),
            pltpu.VMEM((groups, tl, d), BF16),
            pltpu.VMEM((groups, tl, d), BF16),
            dma((3, nb)),
            dma((2,)),
            dma((2,)),
            dma((chunks,)),
            dma((2, groups, 2)),
            dma((2, groups, 2)),
            dma((chunks, subs)),
            dma((2, chunks, subs)),
            dma((chunks, subs)),
            dma((chunks, subs)),
            dma((groups,)),
            dma((groups,)),
            dma((groups,)),
            dma((groups,)),
        ],
        compiler_params=pltpu.CompilerParams(
            collective_id=0, has_side_effects=True, vmem_limit_bytes=60 * 2**20
        ),
    )(tokens, out_grad, w_gate, w_up, w_down)


def weight_grads_kernel(x, h, res, g, gi, out_input, out_gate, out_up, out_down):
    nb, fb = res.shape[0], res.shape[3]
    xt = x[...].T
    for b in range(nb):
        cols = pl.ds(b * fb, fb)
        out_gate[:, cols] = jnp.dot(xt, res[b, 1], preferred_element_type=F32).astype(BF16)
        out_up[:, cols] = jnp.dot(xt, res[b, 2], preferred_element_type=F32).astype(BF16)
    out_down[...] = jnp.dot(h[0, 0].T, g[...], preferred_element_type=F32).astype(BF16)

    @pl.when(pl.program_id(0) == 0)
    def _():
        out_input[...] = gi[...]


def weight_grads(tokens, all_grads, results, grad_input):
    t, d = tokens.shape
    nb, _, _, fb = results.shape
    f = nb * fb
    db = d // nb
    return pl.pallas_call(
        weight_grads_kernel,
        grid=(nb,),
        in_specs=[
            pl.BlockSpec((t, db), lambda i: (0, i)),
            pl.BlockSpec((1, 1, t, fb), lambda i: (i, 0, 0, 0)),
            pl.BlockSpec(results.shape, lambda i: (0, 0, 0, 0)),
            pl.BlockSpec((t, d), lambda i: (0, 0)),
            pl.BlockSpec(grad_input.shape, lambda i: (0, 0)),
        ],
        out_specs=[
            pl.BlockSpec(grad_input.shape, lambda i: (0, 0)),
            pl.BlockSpec((db, f), lambda i: (i, 0)),
            pl.BlockSpec((db, f), lambda i: (i, 0)),
            pl.BlockSpec((fb, d), lambda i: (i, 0)),
        ],
        out_shape=[
            jax.ShapeDtypeStruct(grad_input.shape, BF16),
            jax.ShapeDtypeStruct((d, f), BF16),
            jax.ShapeDtypeStruct((d, f), BF16),
            jax.ShapeDtypeStruct((f, d), BF16),
        ],
        compiler_params=pltpu.CompilerParams(vmem_limit_bytes=60 * 2**20),
        cost_estimate=pl.CostEstimate(
            flops=6 * t * d * f, bytes_accessed=6 * d * f + 10 * t * d, transcendentals=0
        ),
    )(tokens, results, results, all_grads, grad_input)


def shards(n, ncol, tokens, out_grad, w_gate, w_up, w_down):
    all_tokens, all_grads, results, grad_input = main_pass(
        n, ncol, tokens, out_grad, w_gate, w_up, w_down
    )
    return tuple(weight_grads(all_tokens, all_grads, results, grad_input))


def solution(mesh):
    return jax.shard_map(
        functools.partial(shards, mesh.shape["row"], mesh.shape["col"]),
        mesh=mesh,
        in_specs=(
            P("col", "row"),
            P("col", "row"),
            P("row", "col"),
            P("row", "col"),
            P("col", "row"),
        ),
        out_specs=(P("col", "row"), P("row", "col"), P("row", "col"), P("col", "row")),
        check_vma=False,
    )
```

```python
import functools

import jax
import jax.numpy as jnp
from jax import lax
from jax.experimental import pallas as pl
from jax.experimental.pallas import tpu as pltpu
from jax.sharding import PartitionSpec as P

BF16 = jnp.bfloat16
F32 = jnp.float32
MESH = pl.DeviceIdType.MESH


def contract(left_array, right_array, left_dim, right_dim):
    return lax.dot_general(
        left_array,
        right_array,
        (((left_dim,), (right_dim,)), ((), ())),
        preferred_element_type=F32,
    )


def swiglu_back(gate_sum, up_sum, hidden_grad):
    logistic = jax.nn.sigmoid(gate_sum)
    active = gate_sum * logistic
    hidden = (active * up_sum).astype(BF16)
    up_grad = (hidden_grad * active).astype(BF16)
    gate_grad = (hidden_grad * up_sum * logistic * (1.0 + gate_sum * (1.0 - logistic))).astype(BF16)
    return (hidden, gate_grad, up_grad)


def xor(a, b, size):
    total, bit = 0, 1
    while bit < size:
        p, q = (a // bit) % 2, (b // bit) % 2
        total = total + bit * (p + q - 2 * p * q)
        bit *= 2
    return total


def main_kernel(
    n, ncol, m, subs,
    x_hbm, g_hbm, wg_hbm, wu_hbm, wd_hbm,
    xa_out, ga_out, res_out, gi_out,
    xa, ga, wg, wu, wd, part, sent, inbox, res, share, pair, rs_src, rs_got,
    w_sem, own_sem, out_sem, res_sem,
    ag_send, ag_recv, re_send, re_recv,
    in_send, in_recv, res_send, res_recv, pair_send, pair_recv, rs_send, rs_recv,
):
    row, col = lax.axis_index("row"), lax.axis_index("col")
    tl = x_hbm.shape[0]
    nb, _, t, fb = res.shape
    groups = ncol // 2
    own = groups - 1
    gr = 2 * tl
    sr = gr // subs
    chunks = groups * nb
    ahead = 2
    core, chip = col % 2, col // 2
    sibling = col + 1 - 2 * core
    half = n // 2
    side = row // half
    place = row + side * (n - 1 - 2 * row)
    inner = row + 1 - 2 * side
    outer = row - 1 + 2 * side
    middle = place == half - 1
    behind = (place + n - 1) // n

    def weight_copies(b):
        cols = pl.ds(pl.multiple_of(b * fb, fb), fb)
        return (
            pltpu.make_async_copy(wg_hbm.at[:, cols], wg.at[b], w_sem.at[0, b]),
            pltpu.make_async_copy(wu_hbm.at[:, cols], wu.at[b], w_sem.at[1, b]),
            pltpu.make_async_copy(wd_hbm.at[cols, :], wd.at[b], w_sem.at[2, b]),
        )

    def distance(v):
        w = (v + 1) % groups
        return xor(w, w // 2, groups)

    def slot_rows(v, c):
        return pl.ds(pl.multiple_of(v * gr + c * tl, tl), tl)

    def rows_from(v, size):
        return pl.ds(pl.multiple_of(v * gr, gr), size)

    def sub_rows(v, s):
        return pl.ds(pl.multiple_of(v * gr + s * sr, sr), sr)

    def member(v, c):
        return (row, xor(chip, distance(v), groups) * 2 + c)

    def own_copy(a):
        src, dst = ((x_hbm, xa), (g_hbm, ga))[a]
        return pltpu.make_async_copy(src, dst.at[slot_rows(own, core), :], own_sem.at[a])

    def gather_copy(a, v, to):
        src, dst = ((x_hbm, xa), (g_hbm, ga))[a]
        return pltpu.make_async_remote_copy(
            src_ref=src,
            dst_ref=dst.at[slot_rows(v, core), :],
            send_sem=ag_send.at[a, v],
            recv_sem=ag_recv.at[a, v],
            device_id=member(v, to),
            device_id_type=MESH,
        )

    def relay_copy(a, v):
        block = (xa, ga)[a].at[slot_rows(v, core), :]
        return pltpu.make_async_remote_copy(
            src_ref=block,
            dst_ref=block,
            send_sem=re_send.at[a, v],
            recv_sem=re_recv.at[a, v],
            device_id=(row, sibling),
            device_id_type=MESH,
        )

    barrier = pltpu.get_barrier_semaphore()
    pl.semaphore_signal(barrier, inc=1, device_id=(row, sibling), device_id_type=MESH)
    for v in range(own):
        pl.semaphore_signal(barrier, inc=1, device_id=member(v, core), device_id_type=MESH)
    pl.semaphore_signal(barrier, inc=1, device_id=(inner, col), device_id_type=MESH)

    @pl.when(place > 0)
    def _():
        pl.semaphore_signal(barrier, inc=1, device_id=(outer, col), device_id_type=MESH)

    for a in range(2):
        own_copy(a).start()
    for i in range(min(ahead, nb)):
        for copy in weight_copies((i + nb - m) % nb):
            copy.start()
    share[...] = jnp.zeros_like(share)

    pl.semaphore_wait(barrier, groups + 1 + behind)

    for a in range(2):
        gather_copy(a, own, 1 - core).start()
    for v in range(own):
        for a in range(2):
            gather_copy(a, v, core).start()
    for a in range(2):
        own_copy(a).wait()
        gather_copy(a, own, 1 - core).wait_recv()

    def spot(k):
        u = (k - m + chunks) % chunks
        return u // nb, u % nb

    def in_copy(slot, k, s):
        v, b = spot(k)
        return pltpu.make_async_remote_copy(
            src_ref=sent.at[b, :, sub_rows(v, s), :],
            dst_ref=inbox.at[slot, b, :, sub_rows(v, s), :],
            send_sem=in_send.at[k, s],
            recv_sem=in_recv.at[slot, k, s],
            device_id=(inner, col),
            device_id_type=MESH,
        )

    def res_copy(k, s):
        v, b = spot(k)
        block = res.at[b, :, sub_rows(v, s), :]
        return pltpu.make_async_remote_copy(
            src_ref=block,
            dst_ref=block,
            send_sem=res_send.at[k, s],
            recv_sem=res_recv.at[k, s],
            device_id=(outer, col),
            device_id_type=MESH,
        )

    def keep_copy(k):
        v, b = spot(k)
        rows = rows_from(v, gr)
        return pltpu.make_async_copy(res.at[b, :, rows, :], res_out.at[b, :, rows, :], res_sem.at[k])

    def out_copy(a):
        return pltpu.make_async_copy((xa, ga)[a], (xa_out, ga_out)[a], out_sem.at[a])

    def pair_copy(v):
        return pltpu.make_async_remote_copy(
            src_ref=share.at[slot_rows(v, 1 - core), :],
            dst_ref=pair.at[v],
            send_sem=pair_send.at[v],
            recv_sem=pair_recv.at[v],
            device_id=(row, sibling),
            device_id_type=MESH,
        )

    def rs_copy(v):
        return pltpu.make_async_remote_copy(
            src_ref=rs_src.at[v],
            dst_ref=rs_got.at[v],
            send_sem=rs_send.at[v],
            recv_sem=rs_recv.at[v],
            device_id=member(v, core),
            device_id_type=MESH,
        )

    def relay(some):
        for v in some:
            for a in range(2):
                gather_copy(a, v, core).wait_recv()
                relay_copy(a, v).start()

    def send_sums(k, s):
        v, b = spot(k)
        for i in range(3):
            sent[b, i, sub_rows(v, s), :] = part[b, i, sub_rows(v, s), :].astype(BF16)
        in_copy((place + 1) // half, k, s).start()

    def multiply(b, rows):
        x, g = xa[rows, :], ga[rows, :]
        part[b, 0, rows, :] = jnp.dot(x, wg[b], preferred_element_type=F32)
        part[b, 1, rows, :] = jnp.dot(x, wu[b], preferred_element_type=F32)
        part[b, 2, rows, :] = contract(g, wd[b], 1, 1)

    def forward(k):
        _, b = spot(k)

        @pl.when(k < nb)
        def _():
            for copy in weight_copies(b):
                copy.wait()

        @pl.when(k < nb - ahead)
        def _():
            for copy in weight_copies((k + ahead + nb - m) % nb):
                copy.start()

        @pl.when(k < m)
        def _():
            multiply(b, rows_from(own, gr))

        @pl.when(k == m)
        def _():
            for v in range(own):
                for a in range(2):
                    relay_copy(a, v).wait_recv()
            for a in range(2):
                out_copy(a).start()

        @pl.when((k >= m) & (k < nb))
        def _():
            multiply(b, pl.ds(0, t))

        @pl.when((k >= nb) & (k < nb + m))
        def _():
            multiply(b, pl.ds(0, t - gr))

    def accumulate(k):
        v, b = spot(k)
        for s in range(subs):
            in_copy(0, k, s).wait_recv()
            for i in range(3):
                part[b, i, sub_rows(v, s), :] += inbox[0, b, i, sub_rows(v, s), :].astype(F32)
            send_sums(k, s)

    def results(k):
        v, b = spot(k)
        for s in range(subs):
            rows = sub_rows(v, s)

            @pl.when(middle)
            def _():
                in_copy(1, k, s).wait_recv()
                values = swiglu_back(
                    *(part[b, i, rows, :] + inbox[1, b, i, rows, :].astype(F32) for i in range(3))
                )
                for i in range(3):
                    res[b, i, rows, :] = values[i]

            @pl.when(place < half - 1)
            def _():
                res_copy(k, s).wait_recv()

            @pl.when(place > 0)
            def _():
                res_copy(k, s).start()

    def add_share(b, rows):
        share[rows, :] += contract(res[b, 1, rows, :], wg[b], 1, 1) + contract(
            res[b, 2, rows, :], wu[b], 1, 1
        )

    def backward(k):
        v, b = spot(k)
        keep_copy(k).start()
        last = v == own - 1
        tail = k >= chunks - (nb - m)

        @pl.when(((v % 2 == 1) & (v < own)) | (last & (b >= nb - m)))
        def _():
            add_share(b, rows_from(v // 2 * 2, 2 * gr))

        @pl.when((last & (b < nb - m)) | tail)
        def _():
            add_share(b, rows_from(v, gr))

    def complete(k, act):
        v, b = spot(k)
        inside = (k >= 0) & (k < chunks)

        @pl.when(inside & (b == nb - 1) & (v % 2 == 1) & (v < own))
        def _():
            act(v - 1)
            act(v)

        @pl.when(inside & (b == nb - 1) & (v == own - 1))
        def _():
            act(v)

    def pair_sum(v):
        pair_copy(v).wait_recv()
        return share[slot_rows(v, core), :] + pair[v]

    def send_pair(v):
        pair_copy(v).start()

    def send_share(v):
        rs_src[v] = pair_sum(v).astype(BF16)
        rs_copy(v).start()

    def drain(k, inside):
        @pl.when(inside)
        def _():
            keep_copy(k).wait()
            for s in range(subs):
                in_copy(0, k, s).wait_send()

            @pl.when(place > 0)
            def _():
                for s in range(subs):
                    res_copy(k, s).wait_send()

    sum_lag = place
    res_lag = half + 1 + 6 * (half - 1 - place)
    steps = chunks + half + 1 + 6 * (half - 1)
    rest = 3
    near = [v for v in range(own) if distance(v) & (distance(v) - 1) == 0]
    far = [v for v in range(own) if v not in near]

    def step(s, carry):
        @pl.when(s == (m - 1) * (1 - behind) + max(m - 3, 0) * behind)
        def _():
            relay(near)

        @pl.when(s == m - behind)
        def _():
            relay(far)

        @pl.when(s < chunks)
        def _():
            forward(s)

            @pl.when(place == 0)
            def _():
                for i in range(subs):
                    send_sums(s, i)

        k = s - sum_lag

        @pl.when((place > 0) & (k >= 0) & (k < chunks))
        def _():
            accumulate(k)

        r = s - res_lag
        complete(r - 1, send_share)

        @pl.when((r >= 0) & (r < chunks))
        def _():
            results(r)
            backward(r)

        complete(r, send_pair)
        drain(r - rest, (r >= rest) & (r < chunks + rest))
        return carry

    lax.fori_loop(0, steps, step, 0)

    send_pair(own)
    total = pair_sum(own)
    for v in range(own):
        rs_copy(v).wait_recv()
        total += rs_got[v].astype(F32)
    gi_out[...] = total.astype(BF16)

    for a in range(2):
        out_copy(a).wait()
        gather_copy(a, own, 1 - core).wait_send()
        for v in range(own):
            gather_copy(a, v, core).wait_send()
            relay_copy(a, v).wait_send()
    for v in range(groups):
        pair_copy(v).wait_send()
        if v < own:
            rs_copy(v).wait_send()

    for k in range(chunks - rest, chunks):
        drain(k, k >= steps - res_lag - rest)


def main_pass(n, ncol, tokens, out_grad, w_gate, w_up, w_down):
    tl, d = tokens.shape
    f = w_gate.shape[1]
    t = tl * ncol
    fb = min(256, f // 2)
    nb = f // fb
    m = max(1, nb * 3 // 4)
    groups, subs = ncol // 2, 2
    chunks = groups * nb
    vmem = pl.BlockSpec(memory_space=pltpu.VMEM)
    hbm = pl.BlockSpec(memory_space=pl.ANY)
    dma = pltpu.SemaphoreType.DMA
    return pl.pallas_call(
        functools.partial(main_kernel, n, ncol, m, subs),
        out_shape=[
            jax.ShapeDtypeStruct((t, d), BF16),
            jax.ShapeDtypeStruct((t, d), BF16),
            jax.ShapeDtypeStruct((nb, 3, t, fb), BF16),
            jax.ShapeDtypeStruct((tl, d), BF16),
        ],
        in_specs=[hbm] * 5,
        out_specs=[hbm, hbm, hbm, vmem],
        scratch_shapes=[
            pltpu.VMEM((t, d), BF16),
            pltpu.VMEM((t, d), BF16),
            pltpu.VMEM((nb, d, fb), BF16),
            pltpu.VMEM((nb, d, fb), BF16),
            pltpu.VMEM((nb, fb, d), BF16),
            pltpu.VMEM((nb, 3, t, fb), F32),
            pltpu.VMEM((nb, 3, t, fb), BF16),
            pltpu.VMEM((2, nb, 3, t, fb), BF16),
            pltpu.VMEM((nb, 3, t, fb), BF16),
            pltpu.VMEM((t, d), F32),
            pltpu.VMEM((groups, tl, d), F32),
            pltpu.VMEM((groups, tl, d), BF16),
            pltpu.VMEM((groups, tl, d), BF16),
            dma((3, nb)),
            dma((2,)),
            dma((2,)),
            dma((chunks,)),
            dma((2, groups)),
            dma((2, groups)),
            dma((2, groups)),
            dma((2, groups)),
            dma((chunks, subs)),
            dma((2, chunks, subs)),
            dma((chunks, subs)),
            dma((chunks, subs)),
            dma((groups,)),
            dma((groups,)),
            dma((groups,)),
            dma((groups,)),
        ],
        compiler_params=pltpu.CompilerParams(
            collective_id=0, has_side_effects=True, vmem_limit_bytes=60 * 2**20
        ),
    )(tokens, out_grad, w_gate, w_up, w_down)


def weight_grads_kernel(x, res, g, gi, out_input, out_gate, out_up, out_down, xt):
    @pl.when(pl.program_id(0) == 0)
    def _():
        xt[...] = x[...].T
        out_input[...] = gi[...]

    out_gate[...] = jnp.dot(xt[...], res[0, 1], preferred_element_type=F32).astype(BF16)
    out_up[...] = jnp.dot(xt[...], res[0, 2], preferred_element_type=F32).astype(BF16)
    out_down[...] = jnp.dot(res[0, 0].T, g[...], preferred_element_type=F32).astype(BF16)


def weight_grads(tokens, all_grads, results, grad_input):
    t, d = tokens.shape
    nb, _, _, fb = results.shape
    f = nb * fb
    whole = lambda a: pl.BlockSpec(a.shape, lambda i: (0, 0))
    return pl.pallas_call(
        weight_grads_kernel,
        grid=(nb,),
        in_specs=[
            whole(tokens),
            pl.BlockSpec((1, 3, t, fb), lambda i: (i, 0, 0, 0)),
            whole(all_grads),
            whole(grad_input),
        ],
        out_specs=[
            whole(grad_input),
            pl.BlockSpec((d, fb), lambda i: (0, i)),
            pl.BlockSpec((d, fb), lambda i: (0, i)),
            pl.BlockSpec((fb, d), lambda i: (i, 0)),
        ],
        out_shape=[
            jax.ShapeDtypeStruct(grad_input.shape, BF16),
            jax.ShapeDtypeStruct((d, f), BF16),
            jax.ShapeDtypeStruct((d, f), BF16),
            jax.ShapeDtypeStruct((f, d), BF16),
        ],
        scratch_shapes=[pltpu.VMEM((d, t), BF16)],
        compiler_params=pltpu.CompilerParams(vmem_limit_bytes=60 * 2**20),
        cost_estimate=pl.CostEstimate(
            flops=6 * t * d * f, bytes_accessed=6 * d * f + 10 * t * d, transcendentals=0
        ),
    )(tokens, results, all_grads, grad_input)


def shards(n, ncol, tokens, out_grad, w_gate, w_up, w_down):
    all_tokens, all_grads, results, grad_input = main_pass(
        n, ncol, tokens, out_grad, w_gate, w_up, w_down
    )
    return tuple(weight_grads(all_tokens, all_grads, results, grad_input))


def solution(mesh):
    return jax.shard_map(
        functools.partial(shards, mesh.shape["row"], mesh.shape["col"]),
        mesh=mesh,
        in_specs=(
            P("col", "row"),
            P("col", "row"),
            P("row", "col"),
            P("row", "col"),
            P("col", "row"),
        ),
        out_specs=(P("col", "row"), P("row", "col"), P("row", "col"), P("col", "row")),
        check_vma=False,
    )
```

```python
import functools

import jax
import jax.numpy as jnp
from jax import lax
from jax.experimental import pallas as pl
from jax.experimental.pallas import tpu as pltpu
from jax.sharding import PartitionSpec as P

BF16 = jnp.bfloat16
F32 = jnp.float32
MESH = pl.DeviceIdType.MESH


def contract(left_array, right_array, left_dim, right_dim):
    return lax.dot_general(
        left_array,
        right_array,
        (((left_dim,), (right_dim,)), ((), ())),
        preferred_element_type=F32,
    )


def swiglu_back(gate_sum, up_sum, hidden_grad):
    logistic = jax.nn.sigmoid(gate_sum)
    active = gate_sum * logistic
    hidden = (active * up_sum).astype(BF16)
    up_grad = (hidden_grad * active).astype(BF16)
    gate_grad = (hidden_grad * up_sum * logistic * (1.0 + gate_sum * (1.0 - logistic))).astype(BF16)
    return (hidden, gate_grad, up_grad)


def xor(a, b, size):
    total, bit = 0, 1
    while bit < size:
        p, q = (a // bit) % 2, (b // bit) % 2
        total = total + bit * (p + q - 2 * p * q)
        bit *= 2
    return total


def main_kernel(
    n, ncol, m,
    x_hbm, g_hbm, wg_hbm, wu_hbm, wd_hbm,
    xt, ga, res, gi_out,
    xa, wg, wu, wd, part, sent, inbox, share, pair, rs_src, rs_got,
    w_sem, own_sem,
    ag_send, ag_recv, re_send, re_recv,
    in_send, in_recv, res_send, res_recv, pair_send, pair_recv, rs_send, rs_recv,
):
    row, col = lax.axis_index("row"), lax.axis_index("col")
    tl = x_hbm.shape[0]
    nb, _, t, fb = res.shape
    db = xt.shape[0] // nb
    groups = ncol // 2
    own = groups - 1
    gr = 2 * tl
    chunks = groups * nb
    ahead = 2
    core, chip = col % 2, col // 2
    sibling = col + 1 - 2 * core
    half = n // 2
    side = row // half
    place = row + side * (n - 1 - 2 * row)
    inner = row + 1 - 2 * side
    outer = row - 1 + 2 * side
    middle = place == half - 1
    behind = (place + n - 1) // n

    def weight_copies(b):
        cols = pl.ds(pl.multiple_of(b * fb, fb), fb)
        return (
            pltpu.make_async_copy(wg_hbm.at[:, cols], wg.at[b], w_sem.at[0, b]),
            pltpu.make_async_copy(wu_hbm.at[:, cols], wu.at[b], w_sem.at[1, b]),
            pltpu.make_async_copy(wd_hbm.at[cols, :], wd.at[b], w_sem.at[2, b]),
        )

    def distance(v):
        w = (v + 1) % groups
        return xor(w, w // 2, groups)

    def slot_rows(v, c):
        return pl.ds(pl.multiple_of(v * gr + c * tl, tl), tl)

    def rows_from(v, size):
        return pl.ds(pl.multiple_of(v * gr, gr), size)

    def member(v, c):
        return (row, xor(chip, distance(v), groups) * 2 + c)

    def own_copy(a):
        src, dst = ((x_hbm, xa), (g_hbm, ga))[a]
        return pltpu.make_async_copy(src, dst.at[slot_rows(own, core), :], own_sem.at[a])

    def gather_copy(a, v, to):
        src, dst = ((x_hbm, xa), (g_hbm, ga))[a]
        return pltpu.make_async_remote_copy(
            src_ref=src,
            dst_ref=dst.at[slot_rows(v, core), :],
            send_sem=ag_send.at[a, v],
            recv_sem=ag_recv.at[a, v],
            device_id=member(v, to),
            device_id_type=MESH,
        )

    def relay_copy(a, v):
        block = (xa, ga)[a].at[slot_rows(v, core), :]
        return pltpu.make_async_remote_copy(
            src_ref=block,
            dst_ref=block,
            send_sem=re_send.at[a, v],
            recv_sem=re_recv.at[a, v],
            device_id=(row, sibling),
            device_id_type=MESH,
        )

    barrier = pltpu.get_barrier_semaphore()
    pl.semaphore_signal(barrier, inc=1, device_id=(row, sibling), device_id_type=MESH)
    for v in range(own):
        pl.semaphore_signal(barrier, inc=1, device_id=member(v, core), device_id_type=MESH)
    pl.semaphore_signal(barrier, inc=1, device_id=(inner, col), device_id_type=MESH)

    @pl.when(place > 0)
    def _():
        pl.semaphore_signal(barrier, inc=1, device_id=(outer, col), device_id_type=MESH)

    for a in range(2):
        own_copy(a).start()
    for i in range(min(ahead, nb)):
        for copy in weight_copies((i + nb - m) % nb):
            copy.start()
    share[...] = jnp.zeros_like(share)

    pl.semaphore_wait(barrier, groups + 1 + behind)

    for a in range(2):
        gather_copy(a, own, 1 - core).start()
    for v in range(own):
        for a in range(2):
            gather_copy(a, v, core).start()
    def spot(k):
        u = (k - m + chunks) % chunks
        return u // nb, u % nb

    def in_copy(slot, k, s):
        v, b = spot(k)
        rows = slot_rows(v, s)
        return pltpu.make_async_remote_copy(
            src_ref=sent.at[b, :, rows, :],
            dst_ref=inbox.at[slot, b, :, rows, :],
            send_sem=in_send.at[k, s],
            recv_sem=in_recv.at[slot, k, s],
            device_id=(inner, col),
            device_id_type=MESH,
        )

    def res_copy(k, s):
        v, b = spot(k)
        block = res.at[b, :, slot_rows(v, s), :]
        return pltpu.make_async_remote_copy(
            src_ref=block,
            dst_ref=block,
            send_sem=res_send.at[k, s],
            recv_sem=res_recv.at[k, s],
            device_id=(outer, col),
            device_id_type=MESH,
        )

    def pair_copy(v):
        return pltpu.make_async_remote_copy(
            src_ref=share.at[slot_rows(v, 1 - core), :],
            dst_ref=pair.at[v],
            send_sem=pair_send.at[v],
            recv_sem=pair_recv.at[v],
            device_id=(row, sibling),
            device_id_type=MESH,
        )

    def rs_copy(v):
        return pltpu.make_async_remote_copy(
            src_ref=rs_src.at[v],
            dst_ref=rs_got.at[v],
            send_sem=rs_send.at[v],
            recv_sem=rs_recv.at[v],
            device_id=member(v, core),
            device_id_type=MESH,
        )

    def relay(some):
        for v in some:
            for a in range(2):
                gather_copy(a, v, core).wait_recv()
                relay_copy(a, v).start()

    def by_parts(k, act):
        for i in range(2):
            act(k, (core + i + k // (chunks - 1)) % 2)

    def send_sums(k, s):
        v, b = spot(k)
        rows = slot_rows(v, s)
        for i in range(3):
            sent[b, i, rows, :] = part[b, i, rows, :].astype(BF16)
        in_copy((place + 1) // half, k, s).start()

    def multiply(b, rows):
        x, g = xa[rows, :], ga[rows, :]
        part[b, 0, rows, :] = jnp.dot(x, wg[b], preferred_element_type=F32)
        part[b, 1, rows, :] = jnp.dot(x, wu[b], preferred_element_type=F32)
        part[b, 2, rows, :] = contract(g, wd[b], 1, 1)

    def fetch(k):
        @pl.when(k < nb)
        def _():
            for copy in weight_copies((k + nb - m) % nb):
                copy.start()

    def forward(k):
        _, b = spot(k)

        @pl.when(k < nb)
        def _():
            for copy in weight_copies(b):
                copy.wait()

        fetch(k + ahead)

        @pl.when(k < m)
        def _():
            multiply(b, rows_from(own, gr))

        early = nb - m

        def arrived(some):
            for v in some:
                for a in range(2):
                    relay_copy(a, v).wait_recv()

        @pl.when(k == m)
        def _():
            arrived(range(1))

        @pl.when((k >= m) & (k < nb))
        def _():
            multiply(b, rows_from(0, gr))

        @pl.when(k == nb)
        def _():
            arrived(range(1, own))

        @pl.when((k >= nb) & (k < nb + m))
        def _():
            multiply(b, pl.ds(0, t - gr))

        @pl.when((k >= nb + m) & (k < nb + m + early))
        def _():
            multiply(b, rows_from(1, t - gr))

        @pl.when((k >= nb + m) & (k < 2 * nb + m))
        def _():
            cols = pl.ds(pl.multiple_of(b * db, db), db)
            xt[cols, :] = xa[:, cols].T

    def accumulate(k, s):
        v, b = spot(k)
        rows = slot_rows(v, s)
        in_copy(0, k, s).wait_recv()
        for i in range(3):
            total = part[b, i, rows, :] + inbox[0, b, i, rows, :].astype(F32)
            part[b, i, rows, :] = total
            sent[b, i, rows, :] = total.astype(BF16)
        in_copy((place + 1) // half, k, s).start()

    def results(k, s):
        v, b = spot(k)
        rows = slot_rows(v, s)

        @pl.when(middle)
        def _():
            in_copy(1, k, s).wait_recv()
            values = swiglu_back(
                *(part[b, i, rows, :] + inbox[1, b, i, rows, :].astype(F32) for i in range(3))
            )
            for i in range(3):
                res[b, i, rows, :] = values[i]

        @pl.when(place < half - 1)
        def _():
            res_copy(k, s).wait_recv()

        @pl.when(place > 0)
        def _():
            res_copy(k, s).start()

    def add_share(b, rows):
        share[rows, :] += contract(res[b, 1, rows, :], wg[b], 1, 1) + contract(
            res[b, 2, rows, :], wu[b], 1, 1
        )

    def backward(k):
        v, b = spot(k)
        last = v == own - 1
        tail = k >= chunks - (nb - m)

        @pl.when(((v % 2 == 1) & (v < own)) | (last & (b >= nb - m)))
        def _():
            add_share(b, rows_from(v // 2 * 2, 2 * gr))

        @pl.when((last & (b < nb - m)) | tail)
        def _():
            add_share(b, rows_from(v, gr))

    def pair_done(k, act):
        v, b = spot(k)

        @pl.when((k >= 0) & (k < chunks) & (b == nb - 1) & (v % 2 == 1) & (v < own))
        def _():
            act(v - 1)
            act(v)

    def last_done(k, act):
        @pl.when(k == chunks - 1 - (nb - m))
        def _():
            act(own - 1)

    def pair_sum(v):
        pair_copy(v).wait_recv()
        return share[slot_rows(v, core), :] + pair[v]

    def send_pair(v):
        pair_copy(v).start()

    def send_share(v):
        rs_src[v] = pair_sum(v).astype(BF16)
        rs_copy(v).start()

    def sent_all(k, s):
        in_copy(0, k, s).wait_send()

        @pl.when(place > 0)
        def _():
            res_copy(k, s).wait_send()

    def drain(k, inside):
        @pl.when(inside)
        def _():
            by_parts(k, sent_all)

    sum_lag = place
    res_lag = half + 1 + 6 * (half - 1 - place)
    steps = chunks + half + 1 + 6 * (half - 1)
    rest = 3
    near = [v for v in range(own) if distance(v) & (distance(v) - 1) == 0]
    far = [v for v in range(own) if v not in near]

    def step(s, carry):
        @pl.when(s == max(m - 1, 1) * (1 - behind) + max(m - 3, 1) * behind)
        def _():
            relay(near)

        @pl.when(s == nb * (1 - behind) + max(m - 1, 1) * behind)
        def _():
            relay(far)

        @pl.when(s < chunks)
        def _():
            forward(s)

            @pl.when(place == 0)
            def _():
                by_parts(s, send_sums)

        k = s - sum_lag

        @pl.when((place > 0) & (k >= 0) & (k < chunks))
        def _():
            by_parts(k, accumulate)

        r = s - res_lag
        pair_done(r - 2, send_share)
        last_done(r - 1, send_share)

        @pl.when((r >= 0) & (r < chunks - 1))
        def _():
            by_parts(r, results)
            backward(r)

        @pl.when(r == chunks - 1)
        def _():
            for i in range(2):
                c = (core + 1 + i) % 2
                results(r, c)
                add_share(nb - m - 1, slot_rows(own, c))
                if i == 0:
                    send_pair(own)

        pair_done(r, send_pair)
        last_done(r, send_pair)
        drain(r - rest, (r >= rest) & (r < chunks + rest))
        return carry

    for copy in weight_copies(nb - m):
        copy.wait()
    fetch(ahead)
    for i in range(2):
        for a in range(2):
            if i == 0:
                own_copy(a).wait()
            else:
                gather_copy(a, own, 1 - core).wait_recv()
        c = (core + i) % 2
        multiply(nb - m, slot_rows(own, c))

        @pl.when(place == 0)
        def _():
            send_sums(0, c)

    lax.fori_loop(1, steps, step, 0)

    total = pair_sum(own)
    for v in range(own):
        rs_copy(v).wait_recv()
        total += rs_got[v].astype(F32)
    gi_out[...] = total.astype(BF16)

    for a in range(2):
        gather_copy(a, own, 1 - core).wait_send()
        for v in range(own):
            gather_copy(a, v, core).wait_send()
            relay_copy(a, v).wait_send()
    for v in range(groups):
        pair_copy(v).wait_send()
        if v < own:
            rs_copy(v).wait_send()

    for k in range(chunks - rest, chunks):
        drain(k, k >= steps - res_lag - rest)


def main_pass(n, ncol, tokens, out_grad, w_gate, w_up, w_down):
    tl, d = tokens.shape
    f = w_gate.shape[1]
    t = tl * ncol
    fb = min(256, f // 2)
    nb = f // fb
    m = max(1, nb * 3 // 4)
    groups, parts = ncol // 2, 2
    chunks = groups * nb
    vmem = pl.BlockSpec(memory_space=pltpu.VMEM)
    hbm = pl.BlockSpec(memory_space=pl.ANY)
    dma = pltpu.SemaphoreType.DMA
    return pl.pallas_call(
        functools.partial(main_kernel, n, ncol, m),
        out_shape=[
            pltpu.VMEM((d, t), BF16),
            pltpu.VMEM((t, d), BF16),
            pltpu.VMEM((nb, 3, t, fb), BF16),
            pltpu.VMEM((tl, d), BF16),
        ],
        in_specs=[hbm] * 5,
        out_specs=[vmem] * 4,
        scratch_shapes=[
            pltpu.VMEM((t, d), BF16),
            pltpu.VMEM((nb, d, fb), BF16),
            pltpu.VMEM((nb, d, fb), BF16),
            pltpu.VMEM((nb, fb, d), BF16),
            pltpu.VMEM((nb, 3, t, fb), F32),
            pltpu.VMEM((nb, 3, t, fb), BF16),
            pltpu.VMEM((2, nb, 3, t, fb), BF16),
            pltpu.VMEM((t, d), F32),
            pltpu.VMEM((groups, tl, d), F32),
            pltpu.VMEM((groups, tl, d), BF16),
            pltpu.VMEM((groups, tl, d), BF16),
            dma((3, nb)),
            dma((2,)),
            dma((2, groups)),
            dma((2, groups)),
            dma((2, groups)),
            dma((2, groups)),
            dma((chunks, parts)),
            dma((2, chunks, parts)),
            dma((chunks, parts)),
            dma((chunks, parts)),
            dma((groups,)),
            dma((groups,)),
            dma((groups,)),
            dma((groups,)),
        ],
        compiler_params=pltpu.CompilerParams(
            collective_id=0, has_side_effects=True, vmem_limit_bytes=54 * 2**20
        ),
    )(tokens, out_grad, w_gate, w_up, w_down)


def weight_grads_kernel(xt, res, g, gi, out_input, out_gate, out_up, out_down):
    @pl.when(pl.program_id(0) == 0)
    def _():
        out_input[...] = gi[...]

    b = pl.program_id(0)
    out_gate[...] = jnp.dot(xt[...], res[b, 1], preferred_element_type=F32).astype(BF16)
    out_up[...] = jnp.dot(xt[...], res[b, 2], preferred_element_type=F32).astype(BF16)
    out_down[...] = jnp.dot(res[b, 0].T, g[...], preferred_element_type=F32).astype(BF16)


def weight_grads(tokens_t, all_grads, results, grad_input):
    d, t = tokens_t.shape
    nb, _, _, fb = results.shape
    f = nb * fb
    whole = lambda a: pl.BlockSpec(a.shape, lambda i: (0, 0))
    vmem = pl.BlockSpec(memory_space=pltpu.VMEM)
    return pl.pallas_call(
        weight_grads_kernel,
        grid=(nb,),
        in_specs=[vmem] * 4,
        out_specs=[
            whole(grad_input),
            pl.BlockSpec((d, fb), lambda i: (0, i)),
            pl.BlockSpec((d, fb), lambda i: (0, i)),
            pl.BlockSpec((fb, d), lambda i: (i, 0)),
        ],
        out_shape=[
            jax.ShapeDtypeStruct(grad_input.shape, BF16),
            jax.ShapeDtypeStruct((d, f), BF16),
            jax.ShapeDtypeStruct((d, f), BF16),
            jax.ShapeDtypeStruct((f, d), BF16),
        ],
        compiler_params=pltpu.CompilerParams(vmem_limit_bytes=40 * 2**20),
        cost_estimate=pl.CostEstimate(
            flops=6 * t * d * f, bytes_accessed=6 * d * f + 10 * t * d, transcendentals=0
        ),
    )(tokens_t, results, all_grads, grad_input)


def shards(n, ncol, tokens, out_grad, w_gate, w_up, w_down):
    tokens_t, all_grads, results, grad_input = main_pass(
        n, ncol, tokens, out_grad, w_gate, w_up, w_down
    )
    return tuple(weight_grads(tokens_t, all_grads, results, grad_input))


def solution(mesh):
    return jax.shard_map(
        functools.partial(shards, mesh.shape["row"], mesh.shape["col"]),
        mesh=mesh,
        in_specs=(
            P("col", "row"),
            P("col", "row"),
            P("row", "col"),
            P("row", "col"),
            P("col", "row"),
        ),
        out_specs=(P("col", "row"), P("row", "col"), P("row", "col"), P("col", "row")),
        check_vma=False,
    )
```

```python
import functools

import jax
import jax.numpy as jnp
from jax import lax
from jax.experimental import pallas as pl
from jax.experimental.pallas import tpu as pltpu
from jax.sharding import PartitionSpec as P

BF16 = jnp.bfloat16
F32 = jnp.float32
MESH = pl.DeviceIdType.MESH


def contract(left_array, right_array, left_dim, right_dim):
    return lax.dot_general(
        left_array,
        right_array,
        (((left_dim,), (right_dim,)), ((), ())),
        preferred_element_type=F32,
    )


def swiglu_back(gate_sum, up_sum, hidden_grad):
    logistic = jax.nn.sigmoid(gate_sum)
    active = gate_sum * logistic
    hidden = (active * up_sum).astype(BF16)
    up_grad = (hidden_grad * active).astype(BF16)
    gate_grad = (hidden_grad * up_sum * logistic * (1.0 + gate_sum * (1.0 - logistic))).astype(BF16)
    return (hidden, gate_grad, up_grad)


def xor(a, b, size):
    total, bit = 0, 1
    while bit < size:
        p, q = (a // bit) % 2, (b // bit) % 2
        total = total + bit * (p + q - 2 * p * q)
        bit *= 2
    return total


def main_kernel(
    n, ncol, m,
    x_hbm, g_hbm, wg_hbm, wu_hbm, wd_hbm,
    xt, ga, res, gi_out,
    xa, wg, wu, wd, part, sent, inbox, share, pair, rs_src, rs_got,
    w_sem, own_sem,
    ag_send, ag_recv, re_send, re_recv,
    in_send, in_recv, res_send, res_recv, pair_send, pair_recv, rs_send, rs_recv,
):
    row, col = lax.axis_index("row"), lax.axis_index("col")
    tl = x_hbm.shape[0]
    nb, _, t, fb = res.shape
    db = xt.shape[0] // nb
    groups = ncol // 2
    own = groups - 1
    gr = 2 * tl
    chunks = groups * nb
    ahead = 1
    core, chip = col % 2, col // 2
    sibling = col + 1 - 2 * core
    half = n // 2
    side = row // half
    place = row + side * (n - 1 - 2 * row)
    inner = row + 1 - 2 * side
    outer = row - 1 + 2 * side
    middle = place == half - 1
    behind = (place + n - 1) // n

    def weight_copies(b):
        cols = pl.ds(pl.multiple_of(b * fb, fb), fb)
        return (
            pltpu.make_async_copy(wg_hbm.at[:, cols], wg.at[b], w_sem.at[0, b]),
            pltpu.make_async_copy(wu_hbm.at[:, cols], wu.at[b], w_sem.at[1, b]),
            pltpu.make_async_copy(wd_hbm.at[cols, :], wd.at[b], w_sem.at[2, b]),
        )

    def distance(v):
        w = (v + 1) % groups
        return xor(w, w // 2, groups)

    def slot_rows(v, c):
        return pl.ds(pl.multiple_of(v * gr + c * tl, tl), tl)

    def rows_from(v, size):
        return pl.ds(pl.multiple_of(v * gr, gr), size)

    def member(v, c):
        return (row, xor(chip, distance(v), groups) * 2 + c)

    def own_copy(a):
        src, dst = ((x_hbm, xa), (g_hbm, ga))[a]
        return pltpu.make_async_copy(src, dst.at[slot_rows(own, core), :], own_sem.at[a])

    def gather_copy(a, v, to):
        src, dst = ((x_hbm, xa), (g_hbm, ga))[a]
        return pltpu.make_async_remote_copy(
            src_ref=src,
            dst_ref=dst.at[slot_rows(v, core), :],
            send_sem=ag_send.at[a, v],
            recv_sem=ag_recv.at[a, v],
            device_id=member(v, to),
            device_id_type=MESH,
        )

    def relay_copy(a, v):
        block = (xa, ga)[a].at[slot_rows(v, core), :]
        return pltpu.make_async_remote_copy(
            src_ref=block,
            dst_ref=block,
            send_sem=re_send.at[a, v],
            recv_sem=re_recv.at[a, v],
            device_id=(row, sibling),
            device_id_type=MESH,
        )

    barrier = pltpu.get_barrier_semaphore()
    pl.semaphore_signal(barrier, inc=1, device_id=(row, sibling), device_id_type=MESH)
    for v in range(own):
        pl.semaphore_signal(barrier, inc=1, device_id=member(v, core), device_id_type=MESH)
    pl.semaphore_signal(barrier, inc=1, device_id=(inner, col), device_id_type=MESH)

    @pl.when(place > 0)
    def _():
        pl.semaphore_signal(barrier, inc=1, device_id=(outer, col), device_id_type=MESH)

    for a in range(2):
        own_copy(a).start()
    for i in range(min(ahead, nb)):
        for copy in weight_copies((i + nb - m) % nb):
            copy.start()
    share[...] = jnp.zeros_like(share)

    pl.semaphore_wait(barrier, groups + 1 + behind)

    for a in range(2):
        gather_copy(a, own, 1 - core).start()
    for v in range(own):
        for a in range(2):
            gather_copy(a, v, core).start()
    def spot(k):
        u = (k - m + chunks) % chunks
        return u // nb, u % nb

    def in_copy(slot, k, s):
        v, b = spot(k)
        rows = slot_rows(v, s)
        return pltpu.make_async_remote_copy(
            src_ref=sent.at[b, :, rows, :],
            dst_ref=inbox.at[slot, b, :, rows, :],
            send_sem=in_send.at[k, s],
            recv_sem=in_recv.at[slot, k, s],
            device_id=(inner, col),
            device_id_type=MESH,
        )

    def res_copy(k, s):
        v, b = spot(k)
        block = res.at[b, :, slot_rows(v, s), :]
        return pltpu.make_async_remote_copy(
            src_ref=block,
            dst_ref=block,
            send_sem=res_send.at[k, s],
            recv_sem=res_recv.at[k, s],
            device_id=(outer, col),
            device_id_type=MESH,
        )

    def pair_copy(v):
        return pltpu.make_async_remote_copy(
            src_ref=share.at[slot_rows(v, 1 - core), :],
            dst_ref=pair.at[v],
            send_sem=pair_send.at[v],
            recv_sem=pair_recv.at[v],
            device_id=(row, sibling),
            device_id_type=MESH,
        )

    def rs_copy(v):
        return pltpu.make_async_remote_copy(
            src_ref=rs_src.at[v],
            dst_ref=rs_got.at[v],
            send_sem=rs_send.at[v],
            recv_sem=rs_recv.at[v],
            device_id=member(v, core),
            device_id_type=MESH,
        )

    def relay(some):
        for v in some:
            for a in range(2):
                gather_copy(a, v, core).wait_recv()
                relay_copy(a, v).start()

    def by_parts(k, act):
        for i in range(2):
            act(k, (core + i + k // (chunks - 1)) % 2)

    def send_sums(k, s):
        v, b = spot(k)
        rows = slot_rows(v, s)
        for i in range(3):
            sent[b, i, rows, :] = part[b, i, rows, :].astype(BF16)
        in_copy((place + 1) // half, k, s).start()

    def multiply(b, rows):
        x, g = xa[rows, :], ga[rows, :]
        part[b, 0, rows, :] = jnp.dot(x, wg[b], preferred_element_type=F32)
        part[b, 1, rows, :] = jnp.dot(x, wu[b], preferred_element_type=F32)
        part[b, 2, rows, :] = contract(g, wd[b], 1, 1)

    def fetch(k):
        @pl.when(k < nb)
        def _():
            for copy in weight_copies((k + nb - m) % nb):
                copy.start()

    def forward(k):
        _, b = spot(k)

        @pl.when(k < nb)
        def _():
            for copy in weight_copies(b):
                copy.wait()

        fetch(k + ahead)

        @pl.when(k < m)
        def _():
            multiply(b, rows_from(own, gr))

        early = nb - m

        def arrived(some):
            for v in some:
                for a in range(2):
                    relay_copy(a, v).wait_recv()

        @pl.when(k == m)
        def _():
            arrived(range(1))

        @pl.when((k >= m) & (k < nb))
        def _():
            multiply(b, rows_from(0, gr))

        @pl.when(k == nb)
        def _():
            arrived(range(1, own))

        @pl.when((k >= nb) & (k < nb + m))
        def _():
            multiply(b, pl.ds(0, t - gr))

        @pl.when((k >= nb + m) & (k < nb + m + early))
        def _():
            multiply(b, rows_from(1, t - gr))

        @pl.when((k >= nb + m) & (k < 2 * nb + m))
        def _():
            cols = pl.ds(pl.multiple_of(b * db, db), db)
            xt[cols, :] = xa[:, cols].T

    def accumulate(k, s):
        v, b = spot(k)
        rows = slot_rows(v, s)
        in_copy(0, k, s).wait_recv()
        for i in range(3):
            total = part[b, i, rows, :] + inbox[0, b, i, rows, :].astype(F32)
            part[b, i, rows, :] = total
            sent[b, i, rows, :] = total.astype(BF16)
        in_copy((place + 1) // half, k, s).start()

    def results(k, s):
        v, b = spot(k)
        rows = slot_rows(v, s)

        @pl.when(middle)
        def _():
            in_copy(1, k, s).wait_recv()
            values = swiglu_back(
                *(part[b, i, rows, :] + inbox[1, b, i, rows, :].astype(F32) for i in range(3))
            )
            for i in range(3):
                res[b, i, rows, :] = values[i]

        @pl.when(place < half - 1)
        def _():
            res_copy(k, s).wait_recv()

        @pl.when(place > 0)
        def _():
            res_copy(k, s).start()

    def add_share(b, rows):
        share[rows, :] += contract(res[b, 1, rows, :], wg[b], 1, 1) + contract(
            res[b, 2, rows, :], wu[b], 1, 1
        )

    def backward(k):
        v, b = spot(k)
        last = v == own - 1
        tail = k >= chunks - (nb - m)

        @pl.when(((v % 2 == 1) & (v < own)) | (last & (b >= nb - m)))
        def _():
            add_share(b, rows_from(v // 2 * 2, 2 * gr))

        @pl.when((last & (b < nb - m)) | tail)
        def _():
            add_share(b, rows_from(v, gr))

    def pair_done(k, act):
        v, b = spot(k)

        @pl.when((k >= 0) & (k < chunks) & (b == nb - 1) & (v % 2 == 1) & (v < own))
        def _():
            act(v - 1)
            act(v)

    def last_done(k, act):
        @pl.when(k == chunks - 1 - (nb - m))
        def _():
            act(own - 1)

    def pair_sum(v):
        pair_copy(v).wait_recv()
        return share[slot_rows(v, core), :] + pair[v]

    def send_pair(v):
        pair_copy(v).start()

    def send_share(v):
        rs_src[v] = pair_sum(v).astype(BF16)
        rs_copy(v).start()

    def sent_all(k, s):
        in_copy(0, k, s).wait_send()

        @pl.when(place > 0)
        def _():
            res_copy(k, s).wait_send()

    def drain(k, inside):
        @pl.when(inside)
        def _():
            by_parts(k, sent_all)

    sum_lag = place
    res_lag = half + 1 + 6 * (half - 1 - place)
    steps = chunks + half + 1 + 6 * (half - 1)
    rest = 3
    near = [v for v in range(own) if distance(v) & (distance(v) - 1) == 0]
    far = [v for v in range(own) if v not in near]

    def step(s, carry):
        @pl.when(s == max(m - 1, 1) * (1 - behind) + max(m - 3, 1) * behind)
        def _():
            relay(near)

        @pl.when(s == nb * (1 - behind) + max(m - 1, 1) * behind)
        def _():
            relay(far)

        @pl.when(s < chunks)
        def _():
            forward(s)

            @pl.when(place == 0)
            def _():
                by_parts(s, send_sums)

        k = s - sum_lag

        @pl.when((place > 0) & (k >= 0) & (k < chunks))
        def _():
            by_parts(k, accumulate)

        r = s - res_lag
        pair_done(r - 2, send_share)
        last_done(r - 1, send_share)

        @pl.when((r >= 0) & (r < chunks - 1))
        def _():
            by_parts(r, results)
            backward(r)

        @pl.when(r == chunks - 1)
        def _():
            for i in range(2):
                c = (core + 1 + i) % 2
                results(r, c)
                add_share(nb - m - 1, slot_rows(own, c))
                if i == 0:
                    send_pair(own)

        pair_done(r, send_pair)
        last_done(r, send_pair)
        drain(r - rest, (r >= rest) & (r < chunks + rest))
        return carry

    for copy in weight_copies(nb - m):
        copy.wait()
    fetch(ahead)
    for i in range(2):
        for a in range(2):
            if i == 0:
                own_copy(a).wait()
            else:
                gather_copy(a, own, 1 - core).wait_recv()
        c = (core + i) % 2
        multiply(nb - m, slot_rows(own, c))

        @pl.when(place == 0)
        def _():
            send_sums(0, c)

    lax.fori_loop(1, steps, step, 0)

    total = pair_sum(own)
    for v in range(own):
        rs_copy(v).wait_recv()
        total += rs_got[v].astype(F32)
    gi_out[...] = total.astype(BF16)

    for a in range(2):
        gather_copy(a, own, 1 - core).wait_send()
        for v in range(own):
            gather_copy(a, v, core).wait_send()
            relay_copy(a, v).wait_send()
    for v in range(groups):
        pair_copy(v).wait_send()
        if v < own:
            rs_copy(v).wait_send()

    for k in range(chunks - rest, chunks):
        drain(k, k >= steps - res_lag - rest)


def main_pass(n, ncol, tokens, out_grad, w_gate, w_up, w_down):
    tl, d = tokens.shape
    f = w_gate.shape[1]
    t = tl * ncol
    fb = min(256, f // 2)
    nb = f // fb
    m = max(1, nb * 3 // 4)
    groups, parts = ncol // 2, 2
    chunks = groups * nb
    vmem = pl.BlockSpec(memory_space=pltpu.VMEM)
    hbm = pl.BlockSpec(memory_space=pl.ANY)
    dma = pltpu.SemaphoreType.DMA
    return pl.pallas_call(
        functools.partial(main_kernel, n, ncol, m),
        out_shape=[
            pltpu.VMEM((d, t), BF16),
            pltpu.VMEM((t, d), BF16),
            pltpu.VMEM((nb, 3, t, fb), BF16),
            pltpu.VMEM((tl, d), BF16),
        ],
        in_specs=[hbm] * 5,
        out_specs=[vmem] * 4,
        scratch_shapes=[
            pltpu.VMEM((t, d), BF16),
            pltpu.VMEM((nb, d, fb), BF16),
            pltpu.VMEM((nb, d, fb), BF16),
            pltpu.VMEM((nb, fb, d), BF16),
            pltpu.VMEM((nb, 3, t, fb), F32),
            pltpu.VMEM((nb, 3, t, fb), BF16),
            pltpu.VMEM((2, nb, 3, t, fb), BF16),
            pltpu.VMEM((t, d), F32),
            pltpu.VMEM((groups, tl, d), F32),
            pltpu.VMEM((groups, tl, d), BF16),
            pltpu.VMEM((groups, tl, d), BF16),
            dma((3, nb)),
            dma((2,)),
            dma((2, groups)),
            dma((2, groups)),
            dma((2, groups)),
            dma((2, groups)),
            dma((chunks, parts)),
            dma((2, chunks, parts)),
            dma((chunks, parts)),
            dma((chunks, parts)),
            dma((groups,)),
            dma((groups,)),
            dma((groups,)),
            dma((groups,)),
        ],
        compiler_params=pltpu.CompilerParams(
            collective_id=0, has_side_effects=True, vmem_limit_bytes=54 * 2**20
        ),
    )(tokens, out_grad, w_gate, w_up, w_down)


def weight_grads_kernel(xt, res, g, gi, out_input, out_gate, out_up, out_down):
    @pl.when(pl.program_id(0) == 0)
    def _():
        out_input[...] = gi[...]

    b = pl.program_id(0)
    out_gate[...] = jnp.dot(xt[...], res[b, 1], preferred_element_type=F32).astype(BF16)
    out_up[...] = jnp.dot(xt[...], res[b, 2], preferred_element_type=F32).astype(BF16)
    out_down[...] = jnp.dot(res[b, 0].T, g[...], preferred_element_type=F32).astype(BF16)


def weight_grads(tokens_t, all_grads, results, grad_input):
    d, t = tokens_t.shape
    nb, _, _, fb = results.shape
    f = nb * fb
    whole = lambda a: pl.BlockSpec(a.shape, lambda i: (0, 0))
    vmem = pl.BlockSpec(memory_space=pltpu.VMEM)
    return pl.pallas_call(
        weight_grads_kernel,
        grid=(nb,),
        in_specs=[vmem] * 4,
        out_specs=[
            whole(grad_input),
            pl.BlockSpec((d, fb), lambda i: (0, i)),
            pl.BlockSpec((d, fb), lambda i: (0, i)),
            pl.BlockSpec((fb, d), lambda i: (i, 0)),
        ],
        out_shape=[
            jax.ShapeDtypeStruct(grad_input.shape, BF16),
            jax.ShapeDtypeStruct((d, f), BF16),
            jax.ShapeDtypeStruct((d, f), BF16),
            jax.ShapeDtypeStruct((f, d), BF16),
        ],
        compiler_params=pltpu.CompilerParams(vmem_limit_bytes=40 * 2**20),
        cost_estimate=pl.CostEstimate(
            flops=6 * t * d * f, bytes_accessed=6 * d * f + 10 * t * d, transcendentals=0
        ),
    )(tokens_t, results, all_grads, grad_input)


def shards(n, ncol, tokens, out_grad, w_gate, w_up, w_down):
    tokens_t, all_grads, results, grad_input = main_pass(
        n, ncol, tokens, out_grad, w_gate, w_up, w_down
    )
    return tuple(weight_grads(tokens_t, all_grads, results, grad_input))


def solution(mesh):
    return jax.shard_map(
        functools.partial(shards, mesh.shape["row"], mesh.shape["col"]),
        mesh=mesh,
        in_specs=(
            P("col", "row"),
            P("col", "row"),
            P("row", "col"),
            P("row", "col"),
            P("col", "row"),
        ),
        out_specs=(P("col", "row"), P("row", "col"), P("row", "col"), P("col", "row")),
        check_vma=False,
    )
```

```python
import functools

import jax
import jax.numpy as jnp
from jax import lax
from jax.experimental import pallas as pl
from jax.experimental.pallas import tpu as pltpu
from jax.sharding import PartitionSpec as P

BF16 = jnp.bfloat16
F32 = jnp.float32
MESH = pl.DeviceIdType.MESH


def contract(left_array, right_array, left_dim, right_dim):
    return lax.dot_general(
        left_array,
        right_array,
        (((left_dim,), (right_dim,)), ((), ())),
        preferred_element_type=F32,
    )


def swiglu_back(gate_sum, up_sum, hidden_grad):
    logistic = jax.nn.sigmoid(gate_sum)
    active = gate_sum * logistic
    hidden = (active * up_sum).astype(BF16)
    up_grad = (hidden_grad * active).astype(BF16)
    gate_grad = (hidden_grad * up_sum * logistic * (1.0 + gate_sum * (1.0 - logistic))).astype(BF16)
    return (hidden, gate_grad, up_grad)


def xor(a, b, size):
    total, bit = 0, 1
    while bit < size:
        p, q = (a // bit) % 2, (b // bit) % 2
        total = total + bit * (p + q - 2 * p * q)
        bit *= 2
    return total


def main_kernel(
    n, ncol, m,
    x_hbm, g_hbm, wg_hbm, wu_hbm, wd_hbm,
    xt, ga, res, gi_out,
    xa, wg, wu, wd, part, sent, inbox, share, pair, rs_src, rs_got,
    w_sem, own_sem,
    ag_send, ag_recv, re_send, re_recv,
    in_send, in_recv, res_send, res_recv, pair_send, pair_recv, rs_send, rs_recv,
):
    row, col = lax.axis_index("row"), lax.axis_index("col")
    tl = x_hbm.shape[0]
    nb, _, t, fb = res.shape
    db = xt.shape[0] // nb
    groups = ncol // 2
    own = groups - 1
    gr = 2 * tl
    chunks = groups * nb
    ahead = 1
    core, chip = col % 2, col // 2
    sibling = col + 1 - 2 * core
    half = n // 2
    side = row // half
    place = row + side * (n - 1 - 2 * row)
    inner = row + 1 - 2 * side
    outer = row - 1 + 2 * side
    middle = place == half - 1
    behind = (place + n - 1) // n

    def weight_copies(b):
        cols = pl.ds(pl.multiple_of(b * fb, fb), fb)
        return (
            pltpu.make_async_copy(wg_hbm.at[:, cols], wg.at[b], w_sem.at[0, b]),
            pltpu.make_async_copy(wu_hbm.at[:, cols], wu.at[b], w_sem.at[1, b]),
            pltpu.make_async_copy(wd_hbm.at[cols, :], wd.at[b], w_sem.at[2, b]),
        )

    def distance(v):
        w = (v + 1) % groups
        return xor(w, w // 2, groups)

    def slot_rows(v, c):
        return pl.ds(pl.multiple_of(v * gr + c * tl, tl), tl)

    def rows_from(v, size):
        return pl.ds(pl.multiple_of(v * gr, gr), size)

    def member(v, c):
        return (row, xor(chip, distance(v), groups) * 2 + c)

    def own_copy(a):
        src, dst = ((x_hbm, xa), (g_hbm, ga))[a]
        return pltpu.make_async_copy(src, dst.at[slot_rows(own, core), :], own_sem.at[a])

    def gather_copy(a, v, to):
        src, dst = ((x_hbm, xa), (g_hbm, ga))[a]
        return pltpu.make_async_remote_copy(
            src_ref=src,
            dst_ref=dst.at[slot_rows(v, core), :],
            send_sem=ag_send.at[a, v],
            recv_sem=ag_recv.at[a, v],
            device_id=member(v, to),
            device_id_type=MESH,
        )

    def relay_copy(a, v):
        block = (xa, ga)[a].at[slot_rows(v, core), :]
        return pltpu.make_async_remote_copy(
            src_ref=block,
            dst_ref=block,
            send_sem=re_send.at[a, v],
            recv_sem=re_recv.at[a, v],
            device_id=(row, sibling),
            device_id_type=MESH,
        )

    barrier = pltpu.get_barrier_semaphore()
    pl.semaphore_signal(barrier, inc=1, device_id=(row, sibling), device_id_type=MESH)
    for v in range(own):
        pl.semaphore_signal(barrier, inc=1, device_id=member(v, core), device_id_type=MESH)
    pl.semaphore_signal(barrier, inc=1, device_id=(inner, col), device_id_type=MESH)

    @pl.when(place > 0)
    def _():
        pl.semaphore_signal(barrier, inc=1, device_id=(outer, col), device_id_type=MESH)

    for a in range(2):
        own_copy(a).start()
    for i in range(min(ahead, nb)):
        for copy in weight_copies((i + nb - m) % nb):
            copy.start()
    share[...] = jnp.zeros_like(share)

    pl.semaphore_wait(barrier, groups + 1 + behind)

    for a in range(2):
        gather_copy(a, own, 1 - core).start()
    for v in range(own):
        for a in range(2):
            gather_copy(a, v, core).start()
    def spot(k):
        u = (k - m + chunks) % chunks
        return u // nb, u % nb

    def in_copy(slot, k, s):
        v, b = spot(k)
        rows = slot_rows(v, s)
        return pltpu.make_async_remote_copy(
            src_ref=sent.at[b, :, rows, :],
            dst_ref=inbox.at[slot, b, :, rows, :],
            send_sem=in_send.at[k, s],
            recv_sem=in_recv.at[slot, k, s],
            device_id=(inner, col),
            device_id_type=MESH,
        )

    def res_copy(k, s):
        v, b = spot(k)
        block = res.at[b, :, slot_rows(v, s), :]
        return pltpu.make_async_remote_copy(
            src_ref=block,
            dst_ref=block,
            send_sem=res_send.at[k, s],
            recv_sem=res_recv.at[k, s],
            device_id=(outer, col),
            device_id_type=MESH,
        )

    def pair_copy(v):
        return pltpu.make_async_remote_copy(
            src_ref=share.at[slot_rows(v, 1 - core), :],
            dst_ref=pair.at[v],
            send_sem=pair_send.at[v],
            recv_sem=pair_recv.at[v],
            device_id=(row, sibling),
            device_id_type=MESH,
        )

    def rs_copy(v):
        return pltpu.make_async_remote_copy(
            src_ref=rs_src.at[v],
            dst_ref=rs_got.at[v],
            send_sem=rs_send.at[v],
            recv_sem=rs_recv.at[v],
            device_id=member(v, core),
            device_id_type=MESH,
        )

    def relay(some):
        for v in some:
            for a in range(2):
                gather_copy(a, v, core).wait_recv()
                relay_copy(a, v).start()

    def by_parts(k, act):
        for i in range(2):
            act(k, (core + i + k // (chunks - 1)) % 2)

    def send_sums(k, s):
        v, b = spot(k)
        rows = slot_rows(v, s)
        for i in range(3):
            sent[b, i, rows, :] = part[b, i, rows, :].astype(BF16)
        in_copy((place + 1) // half, k, s).start()

    def multiply(b, rows):
        x, g = xa[rows, :], ga[rows, :]
        part[b, 0, rows, :] = jnp.dot(x, wg[b], preferred_element_type=F32)
        part[b, 1, rows, :] = jnp.dot(x, wu[b], preferred_element_type=F32)
        part[b, 2, rows, :] = contract(g, wd[b], 1, 1)

    def fetch(k):
        @pl.when(k < nb)
        def _():
            for copy in weight_copies((k + nb - m) % nb):
                copy.start()

    def forward(k):
        _, b = spot(k)

        @pl.when(k < nb)
        def _():
            for copy in weight_copies(b):
                copy.wait()

        fetch(k + ahead)

        @pl.when(k < m)
        def _():
            multiply(b, rows_from(own, gr))

        early = nb - m

        def arrived(some):
            for v in some:
                for a in range(2):
                    relay_copy(a, v).wait_recv()

        @pl.when(k == m)
        def _():
            arrived(range(1))

        @pl.when((k >= m) & (k < nb))
        def _():
            multiply(b, rows_from(0, gr))

        @pl.when(k == nb)
        def _():
            arrived(range(1, own))

        @pl.when((k >= nb) & (k < nb + m))
        def _():
            multiply(b, pl.ds(0, t - gr))

        @pl.when((k >= nb + m) & (k < nb + m + early))
        def _():
            multiply(b, rows_from(1, t - gr))

        @pl.when((k >= nb + m) & (k < 2 * nb + m))
        def _():
            cols = pl.ds(pl.multiple_of(b * db, db), db)
            xt[cols, :] = xa[:, cols].T

    def accumulate(k, s):
        v, b = spot(k)
        rows = slot_rows(v, s)
        in_copy(0, k, s).wait_recv()
        for i in range(3):
            total = part[b, i, rows, :] + inbox[0, b, i, rows, :].astype(F32)
            part[b, i, rows, :] = total
            sent[b, i, rows, :] = total.astype(BF16)
        in_copy((place + 1) // half, k, s).start()

    def results(k, s):
        v, b = spot(k)
        rows = slot_rows(v, s)

        @pl.when(middle)
        def _():
            in_copy(1, k, s).wait_recv()
            values = swiglu_back(
                *(part[b, i, rows, :] + inbox[1, b, i, rows, :].astype(F32) for i in range(3))
            )
            for i in range(3):
                res[b, i, rows, :] = values[i]

        @pl.when(place < half - 1)
        def _():
            res_copy(k, s).wait_recv()

        @pl.when(place > 0)
        def _():
            res_copy(k, s).start()

    def add_share(b, rows):
        share[rows, :] += contract(res[b, 1, rows, :], wg[b], 1, 1) + contract(
            res[b, 2, rows, :], wu[b], 1, 1
        )

    def backward(k):
        v, b = spot(k)
        last = v == own - 1
        tail = k >= chunks - (nb - m)

        @pl.when(((v % 2 == 1) & (v < own)) | (last & (b >= nb - m)))
        def _():
            add_share(b, rows_from(v // 2 * 2, 2 * gr))

        @pl.when((last & (b < nb - m)) | tail)
        def _():
            add_share(b, rows_from(v, gr))

    def pair_done(k, act):
        v, b = spot(k)

        @pl.when((k >= 0) & (k < chunks) & (b == nb - 1) & (v % 2 == 1) & (v < own))
        def _():
            act(v - 1)
            act(v)

    def last_done(k, act):
        @pl.when(k == chunks - 1 - (nb - m))
        def _():
            act(own - 1)

    def pair_sum(v):
        pair_copy(v).wait_recv()
        return share[slot_rows(v, core), :] + pair[v]

    def send_pair(v):
        pair_copy(v).start()

    def send_share(v):
        rs_src[v] = pair_sum(v).astype(BF16)
        rs_copy(v).start()

    def sent_all(k, s):
        in_copy(0, k, s).wait_send()

        @pl.when(place > 0)
        def _():
            res_copy(k, s).wait_send()

    def drain(k, inside):
        @pl.when(inside)
        def _():
            by_parts(k, sent_all)

    sum_lag = place
    res_lag = half + 1 + 6 * (half - 1 - place)
    steps = chunks + half + 1 + 6 * (half - 1)
    rest = 3
    near = [v for v in range(own) if distance(v) & (distance(v) - 1) == 0]
    far = [v for v in range(own) if v not in near]

    def step(s, carry):
        @pl.when(s == max(m - 1, 1) * (1 - behind) + max(m - 3, 1) * behind)
        def _():
            relay(near)

        @pl.when(s == nb * (1 - behind) + max(m - 1, 1) * behind)
        def _():
            relay(far)

        k = s - sum_lag

        @pl.when((place > 0) & (k >= 0) & (k < chunks))
        def _():
            by_parts(k, accumulate)

        r = s - res_lag
        pair_done(r - 2, send_share)
        last_done(r - 1, send_share)

        @pl.when((r >= 0) & (r < chunks - 1))
        def _():
            by_parts(r, results)
            backward(r)

        @pl.when(r == chunks - 1)
        def _():
            for i in range(2):
                c = (core + 1 + i) % 2
                results(r, c)
                add_share(nb - m - 1, slot_rows(own, c))
                if i == 0:
                    send_pair(own)

        pair_done(r, send_pair)
        last_done(r, send_pair)
        @pl.when(s < chunks)
        def _():
            forward(s)

            @pl.when(place == 0)
            def _():
                by_parts(s, send_sums)

        drain(r - rest, (r >= rest) & (r < chunks + rest))
        return carry

    for copy in weight_copies(nb - m):
        copy.wait()
    fetch(ahead)
    for i in range(2):
        for a in range(2):
            if i == 0:
                own_copy(a).wait()
            else:
                gather_copy(a, own, 1 - core).wait_recv()
        c = (core + i) % 2
        multiply(nb - m, slot_rows(own, c))

        @pl.when(place == 0)
        def _():
            send_sums(0, c)

    lax.fori_loop(1, steps, step, 0)

    total = pair_sum(own)
    for v in range(own):
        rs_copy(v).wait_recv()
        total += rs_got[v].astype(F32)
    gi_out[...] = total.astype(BF16)

    for a in range(2):
        gather_copy(a, own, 1 - core).wait_send()
        for v in range(own):
            gather_copy(a, v, core).wait_send()
            relay_copy(a, v).wait_send()
    for v in range(groups):
        pair_copy(v).wait_send()
        if v < own:
            rs_copy(v).wait_send()

    for k in range(chunks - rest, chunks):
        drain(k, k >= steps - res_lag - rest)


def main_pass(n, ncol, tokens, out_grad, w_gate, w_up, w_down):
    tl, d = tokens.shape
    f = w_gate.shape[1]
    t = tl * ncol
    fb = min(256, f // 2)
    nb = f // fb
    m = max(1, nb * 3 // 4)
    groups, parts = ncol // 2, 2
    chunks = groups * nb
    vmem = pl.BlockSpec(memory_space=pltpu.VMEM)
    hbm = pl.BlockSpec(memory_space=pl.ANY)
    dma = pltpu.SemaphoreType.DMA
    return pl.pallas_call(
        functools.partial(main_kernel, n, ncol, m),
        out_shape=[
            pltpu.VMEM((d, t), BF16),
            pltpu.VMEM((t, d), BF16),
            pltpu.VMEM((nb, 3, t, fb), BF16),
            pltpu.VMEM((tl, d), BF16),
        ],
        in_specs=[hbm] * 5,
        out_specs=[vmem] * 4,
        scratch_shapes=[
            pltpu.VMEM((t, d), BF16),
            pltpu.VMEM((nb, d, fb), BF16),
            pltpu.VMEM((nb, d, fb), BF16),
            pltpu.VMEM((nb, fb, d), BF16),
            pltpu.VMEM((nb, 3, t, fb), F32),
            pltpu.VMEM((nb, 3, t, fb), BF16),
            pltpu.VMEM((2, nb, 3, t, fb), BF16),
            pltpu.VMEM((t, d), F32),
            pltpu.VMEM((groups, tl, d), F32),
            pltpu.VMEM((groups, tl, d), BF16),
            pltpu.VMEM((groups, tl, d), BF16),
            dma((3, nb)),
            dma((2,)),
            dma((2, groups)),
            dma((2, groups)),
            dma((2, groups)),
            dma((2, groups)),
            dma((chunks, parts)),
            dma((2, chunks, parts)),
            dma((chunks, parts)),
            dma((chunks, parts)),
            dma((groups,)),
            dma((groups,)),
            dma((groups,)),
            dma((groups,)),
        ],
        compiler_params=pltpu.CompilerParams(
            collective_id=0, has_side_effects=True, vmem_limit_bytes=54 * 2**20
        ),
    )(tokens, out_grad, w_gate, w_up, w_down)


def weight_grads_kernel(xt, res, g, gi, out_input, out_gate, out_up, out_down):
    @pl.when(pl.program_id(0) == 0)
    def _():
        out_input[...] = gi[...]

    b = pl.program_id(0)
    out_gate[...] = jnp.dot(xt[...], res[b, 1], preferred_element_type=F32).astype(BF16)
    out_up[...] = jnp.dot(xt[...], res[b, 2], preferred_element_type=F32).astype(BF16)
    out_down[...] = jnp.dot(res[b, 0].T, g[...], preferred_element_type=F32).astype(BF16)


def weight_grads(tokens_t, all_grads, results, grad_input):
    d, t = tokens_t.shape
    nb, _, _, fb = results.shape
    f = nb * fb
    whole = lambda a: pl.BlockSpec(a.shape, lambda i: (0, 0))
    vmem = pl.BlockSpec(memory_space=pltpu.VMEM)
    return pl.pallas_call(
        weight_grads_kernel,
        grid=(nb,),
        in_specs=[vmem] * 4,
        out_specs=[
            whole(grad_input),
            pl.BlockSpec((d, fb), lambda i: (0, i)),
            pl.BlockSpec((d, fb), lambda i: (0, i)),
            pl.BlockSpec((fb, d), lambda i: (i, 0)),
        ],
        out_shape=[
            jax.ShapeDtypeStruct(grad_input.shape, BF16),
            jax.ShapeDtypeStruct((d, f), BF16),
            jax.ShapeDtypeStruct((d, f), BF16),
            jax.ShapeDtypeStruct((f, d), BF16),
        ],
        compiler_params=pltpu.CompilerParams(vmem_limit_bytes=40 * 2**20),
        cost_estimate=pl.CostEstimate(
            flops=6 * t * d * f, bytes_accessed=6 * d * f + 10 * t * d, transcendentals=0
        ),
    )(tokens_t, results, all_grads, grad_input)


def shards(n, ncol, tokens, out_grad, w_gate, w_up, w_down):
    tokens_t, all_grads, results, grad_input = main_pass(
        n, ncol, tokens, out_grad, w_gate, w_up, w_down
    )
    return tuple(weight_grads(tokens_t, all_grads, results, grad_input))


def solution(mesh):
    return jax.shard_map(
        functools.partial(shards, mesh.shape["row"], mesh.shape["col"]),
        mesh=mesh,
        in_specs=(
            P("col", "row"),
            P("col", "row"),
            P("row", "col"),
            P("row", "col"),
            P("col", "row"),
        ),
        out_specs=(P("col", "row"), P("row", "col"), P("row", "col"), P("col", "row")),
        check_vma=False,
    )
```
